32 devices in a mesh: row: 8 (over z, y), col: 4 (over x, core).
Axes of the slice: x: 2, y: 2, z: 4, core: 2. Of those that a mesh axis runs over, the one named last changes fastest.
Arguments:
- layer_input: bfloat16 [1024, 12288], P(None, 'row'), may hold values from -6 to 6
- hidden_pre: bfloat16 [1024, 24576], P(None, 'col'), may hold values from -6 to 6
- out_grad: bfloat16 [1024, 12288], P(None, 'row'), may hold values from -8 to 8
- w_up: bfloat16 [12288, 24576], P('row', 'col'), may hold values from -0.0546875 to 0.0546875
- w_down: bfloat16 [24576, 12288], P('col', 'row'), may hold values from -0.0390625 to 0.0390625
Outputs:
- in_grad: bfloat16 [1024, 12288], P('col', 'row')
- up_grad: bfloat16 [12288, 24576], P('row', 'col')
- down_grad: bfloat16 [24576, 12288], P('col', 'row')
The draws below stay inside these ranges and needn't reach their ends.
All inputs are finite; a program needn't handle non-finite values.
Results may differ from the reference program's by a relative error of at most 0.0051.
Values may be sent and summed in bfloat16 or wider, within the bound.
A program may use at most 320 MiB of HBM per device.

```python
import jax
import jax.numpy as jnp

D = 12288
FW = 24576
TOKENS = 1024


def with_spikes(values, own_key, source, target, shards_of, factor):
    owner, partner = [(jnp.arange(values.shape[position]) // (values.shape[position] // shards_of)).reshape([-1 if axis == position else 1 for axis in range(values.ndim)]) for position in (source, target)]
    chosen = jax.random.permutation(own_key, shards_of)[partner]
    strong = (owner == chosen) | (owner == (partner + shards_of // 2) % shards_of)
    return jnp.where(strong, factor * values, values)


def block_scale(key, shape, split, smallest, top_value):
    def one(axis_at, shards_of):
        draws = jax.random.uniform(jax.random.fold_in(jax.random.fold_in(key, 6), axis_at), (shards_of,), jnp.float32, smallest / len(split), top_value / len(split))
        return jnp.repeat(jnp.exp(draws), shape[axis_at] // shards_of).reshape((-1,) + (1,) * (len(shape) - axis_at - 1))

    gain = one(*split[0])
    for cut in split[1:]:
        gain = gain * one(*cut)
    return gain


def noise(rng, shape, width, limit, split=(), kind=jnp.bfloat16):
    factor_of = block_scale(rng, shape, split, -0.22, 0.18) if split else 1.0
    result = jax.random.normal(rng, shape, jnp.float32) * width * factor_of
    return jnp.minimum(jnp.maximum(result, -limit), limit).astype(kind)


def bell_draw_with(stream_key, extent, scale, most, shards, heavy, kind=jnp.bfloat16):
    result = scale * jax.random.normal(stream_key, extent, jnp.float32)
    if shards:
        result = result * block_scale(stream_key, extent, shards, -0.22, 0.18)
    return jnp.clip(with_spikes(result, jax.random.fold_in(stream_key, 3), *heavy), -most, most).astype(kind)


def setup_inputs(seed: int = 0) -> dict:
    seeds = jax.random.split(jax.random.key(seed), 6)
    return {
        "layer_input": noise(seeds[0], (TOKENS, D), 1.0, 6.0, ((1, 8),)),
        "hidden_pre": noise(seeds[1], (TOKENS, FW), 1.0, 6.0, ((1, 4),)),
        "out_grad": bell_draw_with(seeds[2], (TOKENS, D), 1.0, 8.0, ((1, 8),), (1, 0, 8, 2.0)),
        "w_up": noise(seeds[3], (D, FW), D ** -0.5, 0.0546875, ((0, 8), (1, 4))),
        "w_down": noise(seeds[4], (FW, D), FW ** -0.5, 0.0390625, ((0, 4), (1, 8))),
    }


GELU_COEF = 0.7978845608
CUBIC_COEF = 0.044715


def gelu_value(pre_act):
    inner = GELU_COEF * (pre_act + CUBIC_COEF * pre_act * pre_act * pre_act)
    return 0.5 * pre_act * (1.0 + jnp.tanh(inner))


def gelu_slope(pre_act):
    inner = GELU_COEF * (pre_act + CUBIC_COEF * pre_act * pre_act * pre_act)
    tangent = jnp.tanh(inner)
    return 0.5 * (1.0 + tangent) + 0.5 * pre_act * (1.0 - tangent * tangent) * GELU_COEF * (1.0 + 3.0 * CUBIC_COEF * pre_act * pre_act)


def reference(layer_input, hidden_pre, out_grad, w_up, w_down):
    pre_act = hidden_pre.astype(jnp.float32)
    scaling = TOKENS ** -0.5
    activated = gelu_value(pre_act).astype(jnp.bfloat16)
    hidden_sum = jnp.dot(out_grad, w_down.T, preferred_element_type=jnp.float32)
    hidden_grad = (hidden_sum * gelu_slope(pre_act)).astype(jnp.bfloat16)
    in_grad = jnp.dot(hidden_grad, w_up.T, preferred_element_type=jnp.float32).astype(jnp.bfloat16)
    up_grad = (jnp.dot(layer_input.T, hidden_grad, preferred_element_type=jnp.float32) * scaling).astype(jnp.bfloat16)
    down_grad = (jnp.dot(activated.T, out_grad, preferred_element_type=jnp.float32) * scaling).astype(jnp.bfloat16)
    return in_grad, up_grad, down_grad
```

```python
import math

import jax
import jax.numpy as jnp
from jax import lax
from jax.sharding import PartitionSpec as P

GELU_COEF = 0.7978845608
CUBIC_COEF = 0.044715
CONTRACT_LAST = (((1,), (1,)), ((), ()))
CONTRACT_FIRST = (((0,), (0,)), ((), ()))
CHUNKS = 8


def gelu_value(pre_act):
    inner = GELU_COEF * (pre_act + CUBIC_COEF * pre_act * pre_act * pre_act)
    return 0.5 * pre_act * (1.0 + jnp.tanh(inner))


def gelu_slope(pre_act):
    inner = GELU_COEF * (pre_act + CUBIC_COEF * pre_act * pre_act * pre_act)
    tangent = jnp.tanh(inner)
    return 0.5 * (1.0 + tangent) + 0.5 * pre_act * (1.0 - tangent * tangent) * GELU_COEF * (
        1.0 + 3.0 * CUBIC_COEF * pre_act * pre_act
    )


def swap(value, axis_name, size, bit):
    return lax.ppermute(value, axis_name, [(i, i ^ (1 << bit)) for i in range(size)])


def flip_bits(position, bits):
    return sum(((position >> (bits - 1 - b)) & 1) << b for b in range(bits))


def body(rows, cols, layer_input, hidden_pre, out_grad, w_up, w_down):
    tokens = out_grad.shape[0]
    hidden = hidden_pre.shape[1]
    width = out_grad.shape[1]
    row_bits, col_bits = rows.bit_length() - 1, cols.bit_length() - 1
    scaling = 1.0 / math.sqrt(tokens)
    row, col = lax.axis_index("row"), lax.axis_index("col")
    block = tokens // rows
    step = hidden // CHUNKS

    def relative(value):
        parts = [
            lax.dynamic_slice_in_dim(value, (flip_bits(p, row_bits) ^ row) * block, block, 0)
            for p in range(rows)
        ]
        return jnp.concatenate(parts, 0)

    grad_rel = relative(out_grad)
    input_rel = relative(layer_input)
    own_pre = lax.dynamic_slice_in_dim(hidden_pre, row * block, block, 0)

    in_partial = None
    up_grad = jnp.zeros((width, hidden), jnp.bfloat16)
    ups = []
    for c in range(CHUNKS):
        lo, hi = c * step, (c + 1) * step
        weights = w_down[lo:hi]
        half = tokens // 2
        sent = lax.dot_general(
            grad_rel[half:], weights, CONTRACT_LAST, preferred_element_type=jnp.float32
        ).astype(jnp.bfloat16)
        kept = lax.dot_general(
            grad_rel[:half], weights, CONTRACT_LAST, preferred_element_type=jnp.float32
        )
        for bit in range(row_bits):
            got = swap(sent, "row", rows, bit).astype(jnp.float32)
            total = kept + got
            half = total.shape[0] // 2
            if bit + 1 < row_bits:
                kept, sent = total[:half], total[half:].astype(jnp.bfloat16)
        grad = (total * gelu_slope(own_pre[:, lo:hi].astype(jnp.float32))).astype(jnp.bfloat16)
        for bit in reversed(range(row_bits)):
            grad = jnp.concatenate([grad, swap(grad, "row", rows, bit)], 0)
        piece = lax.dot_general(
            grad, w_up[:, lo:hi], CONTRACT_LAST, preferred_element_type=jnp.float32
        )
        in_partial = piece if in_partial is None else in_partial + piece
        up = lax.dot_general(input_rel, grad, CONTRACT_FIRST, preferred_element_type=jnp.float32)
        up_grad = lax.dynamic_update_slice(up_grad, (up * scaling).astype(jnp.bfloat16), (0, lo))

    pre_act = hidden_pre.astype(jnp.float32)
    activated = gelu_value(pre_act).astype(jnp.bfloat16)
    down_total = lax.dot_general(
        activated, out_grad, CONTRACT_FIRST, preferred_element_type=jnp.float32
    )
    down_grad = (down_total * scaling).astype(jnp.bfloat16)

    small = tokens // max(rows, cols)
    per_row, per_col = block // small, tokens // cols // small
    parts = []
    for p in range(cols):
        target = flip_bits(p, col_bits) ^ col
        for k in range(per_col):
            index = target * per_col + k
            place = flip_bits((index // per_row) ^ row, row_bits) * per_row + index % per_row
            parts.append(lax.dynamic_slice_in_dim(in_partial, place * small, small, 0))
    total = jnp.concatenate(parts, 0)
    for bit in range(col_bits):
        half = total.shape[0] // 2
        got = swap(total[half:].astype(jnp.bfloat16), "col", cols, bit).astype(jnp.float32)
        total = total[:half] + got
    return (total.astype(jnp.bfloat16), up_grad, down_grad)


def solution(mesh):
    rows, cols = mesh.shape["row"], mesh.shape["col"]
    placed = (P(None, "row"), P(None, "col"), P(None, "row"), P("row", "col"), P("col", "row"))
    return jax.shard_map(
        lambda *args: body(rows, cols, *args),
        mesh=mesh,
        in_specs=placed,
        out_specs=(P("col", "row"), P("row", "col"), P("col", "row")),
        check_vma=False,
    )
```
